32 devices in a mesh: row: 8 (over y, x, core), col: 4 (over z).
Axes of the slice: x: 2, y: 2, z: 4, core: 2. Of those that a mesh axis runs over, the one named last changes fastest.
Arguments:
- trial_vectors: bfloat16 [6144, 256], P(('row', 'col')), may hold values from -6 to 6
- h_blocks: bfloat16 [4, 8, 12, 64, 8, 128], P('col', None, None, None, 'row'), may hold values from -0.1875 to 0.1875
- block_col: int32 [4, 8, 12, 8, 2], P('col', 'row'), may hold values from 0 to 2
- block_count: int32 [4, 8, 12, 8], P('col', 'row'), may hold values from 0 to 2, as said below
- center: float32 [1], replicated, may hold values from -0.5 to 0.5
- half_width: float32 [1], replicated, may hold values from 1.5 to 2.5
Outputs:
- filtered: float32 [6144, 256], P(('row', 'col'))
The draws below stay inside these ranges and needn't reach their ends.
Inputs may be any that keep to these rules, and one draw needn't show every extreme that they name: Only the first block_count slots of a block row and source domain hold blocks. In every column group one row domain has all 2 slots used in every block row for every source domain.
All inputs are finite; a program needn't handle non-finite values.
Results may differ from the reference program's by a relative error of at most 0.019.
Values may be sent and summed in bfloat16 or wider, within the bound.
No kernel may reach another device: no remote copies, remote signals or barrier semaphores. Data moves between devices by JAX's collectives and lax.ppermute only.
A program may use at most 64 MiB of HBM per device.

```python
import jax
import jax.numpy as jnp
from jax import lax

BLOCK = 64
VECTORS = 256
PER = 2
DEGREE = 6
BLOCK_ROWS = 3
DOMAIN_ROWS = 12
ORBITALS = 6144
N_ROW = 8
N_COL = 4


def draw_block_count(key, part):
    first, second = jax.random.split(jax.random.fold_in(key, 23))
    target = jnp.arange(N_ROW).astype(jnp.int32)[:, None, None]
    source = jnp.arange(N_ROW).astype(jnp.int32)[None, None, :]
    spacing = jnp.abs(target - source)
    apart = jnp.minimum(spacing, N_ROW - spacing)
    base = jax.random.randint(first, (N_COL, N_ROW, DOMAIN_ROWS, N_ROW), 0, PER + 1)
    counts = jnp.minimum(PER, base * 4 // (2 + apart))
    chosen = jax.random.randint(second, (N_COL, 1, 1, 1), 0, N_ROW)
    counts = jnp.where(target[None] == chosen, PER, counts)
    return counts.astype(jnp.int32)


def touch_ends(drawn, stream_key, least, top_value):
    longest = drawn.shape.index(max(drawn.shape))
    spots = []
    for shift in (0, 1):
        where = [jax.random.randint(jax.random.fold_in(stream_key, axis), (), 0, length) for axis, length in enumerate(drawn.shape)]
        where[longest] = (where[longest] + shift) % drawn.shape[longest]
        spots.append(tuple(where))
    return drawn.at[spots[0]].set(least).at[spots[1]].set(top_value)


def levels(own_key, extent, cuts, smallest, top_value):
    factor_of = 1.0
    for axis_at, parts in cuts:
        draws = jax.random.uniform(jax.random.fold_in(jax.random.fold_in(own_key, 6), axis_at), (parts,), jnp.float32, smallest / len(cuts), top_value / len(cuts))
        factor_of = factor_of * jnp.repeat(jnp.exp(draws), extent[axis_at] // parts).reshape((-1,) + (1,) * (len(extent) - 1 - axis_at))
    return factor_of


def scatter_about(key, extent, scale, reach, cuts=(), kind=jnp.bfloat16):
    array = jax.random.normal(key, extent, jnp.float32) * scale
    if len(cuts) > 0:
        array = levels(key, extent, cuts, -0.22, 0.18) * array
    return jnp.clip(array, min=-reach, max=reach).astype(kind)


def setup_inputs(seed: int = 0) -> dict:
    splits = jax.random.split(jax.random.key(seed), 7)
    trial_vectors = scatter_about(splits[0], (ORBITALS, VECTORS), 1.0, 6.0, ((0, 32),))
    h_blocks = scatter_about(splits[1], (N_COL, N_ROW, DOMAIN_ROWS, BLOCK, N_ROW, PER * BLOCK), (N_COL * N_ROW * PER * BLOCK // 4) ** -0.5, 0.1875, ((0, 4), (4, 8)))
    block_col = touch_ends(jax.random.randint(splits[2], (N_COL, N_ROW, DOMAIN_ROWS, N_ROW, PER), 0, BLOCK_ROWS), jax.random.fold_in(splits[2], 1), 0, BLOCK_ROWS - 1).astype(jnp.int32)
    block_count = draw_block_count(jax.random.fold_in(splits[6], 71), 0)
    center = jnp.clip(jax.random.uniform(splits[4], (1,), jnp.float32, -0.5, 0.5), -0.5, 0.5)
    half_width = jnp.clip(jax.random.uniform(splits[5], (1,), jnp.float32, 1.5, 2.5), 1.5, 2.5)
    return {"trial_vectors": trial_vectors, "h_blocks": h_blocks, "block_col": block_col, "block_count": block_count, "center": center, "half_width": half_width}


def apply_operator(panel, h_blocks, block_col, block_count):
    domain = BLOCK_ROWS * N_COL
    contraction = N_ROW * PER * BLOCK
    xblocks = lax.optimization_barrier(panel).reshape(N_ROW * domain, BLOCK, VECTORS)
    slot_index = jnp.arange(PER, dtype=jnp.int32)
    source_index = jnp.arange(N_ROW, dtype=jnp.int32)

    def one_domain(group_index, domain_index):
        filled = slot_index[None, None, :] < block_count[group_index, domain_index][:, :, None]
        raw_blocks = h_blocks[group_index, domain_index].reshape(domain, BLOCK, N_ROW, PER, BLOCK)
        masked = jnp.where(filled[:, None, :, :, None], raw_blocks, jnp.zeros((), raw_blocks.dtype))
        masked = masked.reshape(domain, BLOCK, contraction)
        columns = (source_index[None, :, None] * N_COL + group_index) * BLOCK_ROWS + block_col[group_index, domain_index]
        columns = columns.reshape(domain, N_ROW * PER).astype(jnp.int32)
        picked = xblocks[columns].reshape(domain, contraction, VECTORS)
        return jnp.einsum("rak,rkv->rav", masked.astype(jnp.float32), picked.astype(jnp.float32))

    def per_group(summed, group_index):
        sums = lax.map(lambda domain_index: one_domain(group_index, domain_index), jnp.arange(N_ROW, dtype=jnp.int32))
        rounded = lax.optimization_barrier(sums.astype(jnp.bfloat16))
        return summed + rounded.astype(jnp.float32), None

    summed, _ = lax.scan(per_group, jnp.zeros((N_ROW, domain, BLOCK, VECTORS), jnp.float32), jnp.arange(N_COL, dtype=jnp.int32))
    return summed.reshape(N_ROW * domain * BLOCK, VECTORS)


def reference(trial_vectors, h_blocks, block_col, block_count, center, half_width):
    centre_value = center[0]
    half_value = half_width[0]
    previous = trial_vectors.astype(jnp.float32)
    current = (apply_operator(trial_vectors, h_blocks, block_col, block_count) - centre_value * previous) / half_value
    for degree_step in range(DEGREE - 1):
        panel_now = current.astype(jnp.bfloat16)
        product = apply_operator(panel_now, h_blocks, block_col, block_count)
        following = 2.0 * (product - centre_value * current) / half_value - previous
        previous, current = current, following
    return current
```

```python
import functools

import jax
import jax.numpy as jnp
from jax import lax
from jax.experimental import pallas as pl
from jax.experimental.pallas import tpu as pltpu
from jax.sharding import PartitionSpec as P

DEGREE = 6
PAIR = 2


def exchange(value, axis, size, offset):
    return lax.ppermute(value, axis, [(i, i ^ offset) for i in range(size)])


def place_blocks(step, per, width, rows, place, used, same, other, dense):
    near = pl.program_id(0) % PAIR
    piece = place[2] ^ (pl.program_id(0) // PAIR)
    sources = place[4]
    chip = place[0] ^ step
    lane = lax.broadcasted_iota(jnp.int32, (1, PAIR * width), 1) < width
    count = rows // width
    for row in range(count):
        here = pl.ds(row * width, width)
        base = (near * place[3] + piece) * count + row
        sides = []
        for far, ref in enumerate((same, other)):
            value = ref[0, here, :].astype(jnp.float32)
            turned = pltpu.roll(value, width, 1)
            source = PAIR * chip + (place[1] ^ far)
            slots = [used[(base * sources + source) * PAIR + slot] for slot in range(PAIR)]
            sides.append((value, turned, slots))
        halves = [(far, column) for far in range(PAIR) for column in range(per)]
        for tile in range(len(halves) // 2):
            (far_a, col_a), (far_b, col_b) = halves[2 * tile], halves[2 * tile + 1]
            a, b = sides[far_a], sides[far_b]
            keep = jnp.where(lane, (a[2][0] == col_a).astype(jnp.float32), (b[2][1] == col_b).astype(jnp.float32))
            swap = jnp.where(lane, (a[2][1] == col_a).astype(jnp.float32), (b[2][0] == col_b).astype(jnp.float32))
            straight = a[0] if far_a == far_b else jnp.where(lane, a[0], b[0])
            turned = a[1] if far_a == far_b else jnp.where(lane, a[1], b[1])
            dense[here, pl.ds(tile * PAIR * width, PAIR * width)] = (straight * keep + turned * swap).astype(dense.dtype)


def body(per, trial_vectors, h_blocks, block_col, block_count, center, half_width):
    row_count = lax.axis_size("row")
    col_count = lax.axis_size("col")
    chips = row_count // PAIR
    row_index = lax.axis_index("row")
    chip, core = row_index // PAIR, row_index % PAIR
    piece = lax.axis_index("col")
    domain = h_blocks.shape[2]
    width = h_blocks.shape[3]
    slots = h_blocks.shape[5] // width
    vectors = trial_vectors.shape[1] // PAIR

    raw = h_blocks.reshape(row_count, domain * width, slots * width)
    used = jnp.where(
        lax.broadcasted_iota(jnp.int32, block_col.shape[2:], 2) < block_count[0, 0][:, :, None],
        block_col[0, 0],
        -1,
    ).reshape(-1)
    used = jnp.concatenate([used, exchange(used, "row", row_count, 1)])

    first = trial_vectors[:, :vectors]
    second = trial_vectors[:, vectors:]
    mine = jnp.where(core == 0, first, second)
    theirs = exchange(jnp.where(core == 0, second, first), "row", row_count, 1)
    panel = jnp.concatenate([mine, theirs])

    place = jnp.stack([chip, core, piece, jnp.int32(col_count), jnp.int32(row_count)]).astype(jnp.int32)
    rows = domain * width // col_count
    matrices = []
    for step in range(chips):
        sent = lax.dynamic_slice_in_dim(raw, PAIR * (chip ^ step), PAIR, 0)
        same = sent if step == 0 else exchange(sent, "row", row_count, PAIR * step)
        other = exchange(same, "row", row_count, 1)
        same = same.reshape(PAIR * col_count, rows, slots * width)
        other = other.reshape(PAIR * col_count, rows, slots * width)

        def pick(i, place_ref, used_ref):
            return ((place_ref[1] ^ (i % PAIR)) * place_ref[3] + (place_ref[2] ^ (i // PAIR)), 0, 0)

        block = pl.BlockSpec((1, rows, slots * width), pick)
        columns = PAIR * per * width
        matrices.append(
            pl.pallas_call(
                functools.partial(place_blocks, step, per, width, rows),
                out_shape=jax.ShapeDtypeStruct((PAIR * domain * width, columns), jnp.bfloat16),
                grid_spec=pltpu.PrefetchScalarGridSpec(
                    num_scalar_prefetch=2,
                    grid=(PAIR * col_count,),
                    in_specs=[block, block],
                    out_specs=pl.BlockSpec((rows, columns), lambda i, place_ref, used_ref: (i, 0)),
                ),
                cost_estimate=pl.CostEstimate(
                    flops=PAIR * domain * width * columns * 3,
                    bytes_accessed=PAIR * domain * width * columns * 4,
                    transcendentals=0,
                ),
                name=f"place_{step}",
            )(place, used, same, other)
        )

    centre_value = center[0]
    half_value = half_width[0]
    span = PAIR * rows

    def operator(current):
        total = jnp.dot(matrices[0], current, preferred_element_type=jnp.float32)
        arrived = [exchange(current, "row", row_count, PAIR * step) for step in range(1, chips)]
        for step in range(1, chips):
            total = total + jnp.dot(matrices[step], arrived[step - 1], preferred_element_type=jnp.float32)
        owned = total[:span]
        parts = [
            exchange(total[step * span : (step + 1) * span].astype(jnp.bfloat16), "col", col_count, step)
            for step in range(1, col_count)
        ]
        for part in parts:
            owned = owned + part.astype(jnp.float32)
        return owned

    previous = panel.astype(jnp.float32)
    current = (operator(panel) - centre_value * previous) / half_value
    for degree_step in range(DEGREE - 1):
        product = operator(current.astype(jnp.bfloat16))
        following = 2.0 * (product - centre_value * current) / half_value - previous
        previous, current = (current, following)

    mine, theirs = current[:rows], exchange(current[rows:], "row", row_count, 1)
    return jnp.where(
        core == 0, jnp.concatenate([mine, theirs], 1), jnp.concatenate([theirs, mine], 1)
    )


def solution(mesh):
    in_specs = (
        P(("row", "col"), None),
        P("col", None, None, None, "row", None),
        P("col", "row", None, None, None),
        P("col", "row", None, None),
        P(),
        P(),
    )
    out_specs = P(("row", "col"), None)

    def whole(trial_vectors, h_blocks, block_col, block_count, center, half_width):
        shape = h_blocks.shape
        per = trial_vectors.shape[0] // (shape[0] * shape[4] * shape[3])
        return jax.shard_map(
            functools.partial(body, per), mesh=mesh, in_specs=in_specs, out_specs=out_specs, check_vma=False
        )(trial_vectors, h_blocks, block_col, block_count, center, half_width)

    return whole
```

```python
import functools

import jax
import jax.numpy as jnp
from jax import lax
from jax.experimental import pallas as pl
from jax.experimental.pallas import tpu as pltpu
from jax.sharding import PartitionSpec as P

DEGREE = 6
PAIR = 2
SLOTS = 2
UNROLL = 6


def exchange(value, axis, size, offset):
    return lax.ppermute(value, axis, [(i, i ^ offset) for i in range(size)])


def place_blocks(step, per, width, half, pieces, sources, place, used, same, other, dense):
    chip, core, piece = place[0], place[1], place[2]
    lane = lax.broadcasted_iota(jnp.int32, (1, SLOTS * width), 1) < width
    held = pieces // 2
    count = dense.shape[0] // (held * PAIR * width)
    halves = [(far, column) for far in range(PAIR) for column in range(per)]

    def block_row(index, carry):
        row = lax.rem(index, count)
        near = lax.rem(index // count, PAIR)
        at = (piece ^ (index // (count * PAIR))) & (held - 1)
        base = (near * pieces + (at | (((piece // held) ^ half) * held))) * count + row
        source_row = pl.multiple_of(((core ^ near) * held + at) * count * width + row * width, width)
        sides = []
        for far, ref in enumerate((same, other)):
            value = ref[pl.ds(source_row, width), :]
            source = PAIR * (chip ^ step) + (core ^ far)
            slots = [used[(base * sources + source) * SLOTS + slot] for slot in range(SLOTS)]
            sides.append((value, pltpu.roll(value, width, 1), slots))
        target = pl.multiple_of(index * width, width)
        for tile in range(len(halves) // 2):
            (far_a, col_a), (far_b, col_b) = halves[2 * tile], halves[2 * tile + 1]
            terms = {}
            for far, turned, wanted, left in (
                (far_a, 0, sides[far_a][2][0] == col_a, True),
                (far_a, 1, sides[far_a][2][1] == col_a, True),
                (far_b, 0, sides[far_b][2][1] == col_b, False),
                (far_b, 1, sides[far_b][2][0] == col_b, False),
            ):
                terms.setdefault((far, turned), []).append((wanted.astype(jnp.int32), left))
            result = None
            for (far, turned), wanted in terms.items():
                sides_wanted = {left: value for value, left in wanted}
                factor = jnp.where(lane, sides_wanted.get(True, 0), sides_wanted.get(False, 0))
                term = sides[far][turned] * factor.astype(jnp.float32).astype(dense.dtype)
                result = term if result is None else result + term
            dense[pl.ds(target, width), pl.ds(tile * SLOTS * width, SLOTS * width)] = result
        return carry

    lax.fori_loop(0, held * PAIR * count, block_row, 0, unroll=UNROLL)


def body(per, trial_vectors, h_blocks, block_col, block_count, center, half_width):
    row_count = lax.axis_size("row")
    col_count = lax.axis_size("col")
    chips = row_count // PAIR
    row_index = lax.axis_index("row")
    chip, core = row_index // PAIR, row_index % PAIR
    piece = lax.axis_index("col")
    domain = h_blocks.shape[2]
    width = h_blocks.shape[3]
    slots = h_blocks.shape[5] // width
    vectors = trial_vectors.shape[1] // PAIR

    raw = h_blocks.reshape(row_count, domain * width, slots * width)
    used = jnp.where(
        lax.broadcasted_iota(jnp.int32, block_col.shape[2:], 2) < block_count[0, 0][:, :, None],
        block_col[0, 0],
        -1,
    ).reshape(-1)
    used = jnp.concatenate([used, exchange(used, "row", row_count, 1)])

    first = trial_vectors[:, :vectors]
    second = trial_vectors[:, vectors:]
    mine = jnp.where(core == 0, first, second)
    theirs = exchange(jnp.where(core == 0, second, first), "row", row_count, 1)
    panel = jnp.concatenate([mine, theirs])

    place = jnp.stack([chip, core, piece]).astype(jnp.int32)
    held = col_count // 2
    part = domain * width // 2
    columns = PAIR * per * width
    scalars = pl.BlockSpec(memory_space=pltpu.SMEM)
    vectors_spec = pl.BlockSpec(memory_space=pltpu.VMEM)
    matrices = [[None] * chips for _ in range(2)]
    for half in (1, 0):
        top = (piece // held) ^ half
        for step in range(chips):
            sent = lax.dynamic_slice(
                raw, (PAIR * (chip ^ step), top * part, 0), (PAIR, part, slots * width)
            )
            same = sent if step == 0 else exchange(sent, "row", row_count, PAIR * step)
            other = exchange(same, "row", row_count, 1)
            matrices[half][step] = pl.pallas_call(
                functools.partial(place_blocks, step, per, width, half, col_count, row_count),
                out_shape=jax.ShapeDtypeStruct((PAIR * part, columns), jnp.bfloat16),
                in_specs=[scalars, scalars, vectors_spec, vectors_spec],
                out_specs=vectors_spec,
                cost_estimate=pl.CostEstimate(
                    flops=PAIR * part * columns * 3,
                    bytes_accessed=PAIR * part * columns * 4,
                    transcendentals=0,
                ),
                compiler_params=pltpu.CompilerParams(
                    vmem_limit_bytes=PAIR * part * (columns + 2 * slots * width) * 4 + (1 << 20)
                ),
                name=f"place_{half}_{step}",
            )(
                place,
                used,
                same.reshape(PAIR * part, slots * width),
                other.reshape(PAIR * part, slots * width),
            )

    centre_value = center[0]
    half_value = half_width[0]
    rows = domain * width // col_count
    span = PAIR * rows

    def operator(current):
        arrived = [current] + [
            exchange(current, "row", row_count, PAIR * step) for step in range(1, chips)
        ]
        parts = {}
        for half in (1, 0):
            total = None
            for matrix, value in zip(matrices[half], arrived):
                term = jnp.dot(matrix, value, preferred_element_type=jnp.float32)
                total = term if total is None else total + term
            for index in range(held):
                step = half * held + index
                value = total[index * span : (index + 1) * span]
                parts[step] = (
                    exchange(value.astype(jnp.bfloat16), "col", col_count, step) if step else value
                )
        owned = parts[0]
        for step in range(1, col_count):
            owned = owned + parts[step].astype(jnp.float32)
        return owned

    previous = panel.astype(jnp.float32)
    current = (operator(panel) - centre_value * previous) / half_value
    for degree_step in range(DEGREE - 1):
        product = operator(current.astype(jnp.bfloat16))
        following = 2.0 * (product - centre_value * current) / half_value - previous
        previous, current = (current, following)

    mine, theirs = current[:rows], exchange(current[rows:], "row", row_count, 1)
    return jnp.where(
        core == 0, jnp.concatenate([mine, theirs], 1), jnp.concatenate([theirs, mine], 1)
    )


def solution(mesh):
    in_specs = (
        P(("row", "col"), None),
        P("col", None, None, None, "row", None),
        P("col", "row", None, None, None),
        P("col", "row", None, None),
        P(),
        P(),
    )
    out_specs = P(("row", "col"), None)

    def whole(trial_vectors, h_blocks, block_col, block_count, center, half_width):
        shape = h_blocks.shape
        per = trial_vectors.shape[0] // (shape[0] * shape[4] * shape[3])
        return jax.shard_map(
            functools.partial(body, per), mesh=mesh, in_specs=in_specs, out_specs=out_specs, check_vma=False
        )(trial_vectors, h_blocks, block_col, block_count, center, half_width)

    return whole
```

```python
import functools

import jax
import jax.numpy as jnp
from jax import lax
from jax.experimental import pallas as pl
from jax.experimental.pallas import tpu as pltpu
from jax.sharding import PartitionSpec as P


DEGREE = 6
PAIR = 2
SLOTS = 2
UNROLL = 6


def exchange(value, axis, size, offset):
    return lax.ppermute(value, axis, [(i, i ^ offset) for i in range(size)])


def place_blocks(step, per, width, half, pieces, sources, place, used, same, other, dense):
    chip, core, piece = place[0], place[1], place[2]
    lane = lax.broadcasted_iota(jnp.int32, (1, SLOTS * width), 1) < width
    held = pieces // 2
    count = dense.shape[0] // (held * PAIR * width)
    halves = [(far, column) for far in range(PAIR) for column in range(per)]

    def block_row(index, carry):
        row = lax.rem(index, count)
        near = lax.rem(index // count, PAIR)
        at = (piece ^ (index // (count * PAIR))) & (held - 1)
        base = (near * pieces + (at | (((piece // held) ^ half) * held))) * count + row
        source_row = pl.multiple_of(((core ^ near) * held + at) * count * width + row * width, width)
        sides = []
        for far, ref in enumerate((same, other)):
            value = ref[pl.ds(source_row, width), :]
            source = PAIR * (chip ^ step) + (core ^ far)
            slots = [used[(base * sources + source) * SLOTS + slot] for slot in range(SLOTS)]
            sides.append((value, pltpu.roll(value, width, 1), slots))
        target = pl.multiple_of(index * width, width)
        for tile in range(len(halves) // 2):
            (far_a, col_a), (far_b, col_b) = halves[2 * tile], halves[2 * tile + 1]
            terms = {}
            for far, turned, wanted, left in (
                (far_a, 0, sides[far_a][2][0] == col_a, True),
                (far_a, 1, sides[far_a][2][1] == col_a, True),
                (far_b, 0, sides[far_b][2][1] == col_b, False),
                (far_b, 1, sides[far_b][2][0] == col_b, False),
            ):
                terms.setdefault((far, turned), []).append((wanted.astype(jnp.int32), left))
            result = None
            for (far, turned), wanted in terms.items():
                sides_wanted = {left: value for value, left in wanted}
                factor = jnp.where(lane, sides_wanted.get(True, 0), sides_wanted.get(False, 0))
                term = sides[far][turned] * factor.astype(jnp.float32).astype(dense.dtype)
                result = term if result is None else result + term
            dense[pl.ds(target, width), pl.ds(tile * SLOTS * width, SLOTS * width)] = result
        return carry

    lax.fori_loop(0, held * PAIR * count, block_row, 0, unroll=UNROLL)


def filter_body(per, trial_vectors, h_blocks, block_col, block_count, center, half_width):
    row_count = lax.axis_size("row")
    col_count = lax.axis_size("col")
    chips = row_count // PAIR
    row_index = lax.axis_index("row")
    chip, core = row_index // PAIR, row_index % PAIR
    piece = lax.axis_index("col")
    domain = h_blocks.shape[2]
    width = h_blocks.shape[3]
    slots = h_blocks.shape[5] // width
    vectors = trial_vectors.shape[1] // PAIR

    raw = h_blocks.reshape(row_count, domain * width, slots * width)
    used = jnp.where(
        lax.broadcasted_iota(jnp.int32, block_col.shape[2:], 2) < block_count[0, 0][:, :, None],
        block_col[0, 0],
        -1,
    ).reshape(-1)
    used = jnp.concatenate([used, exchange(used, "row", row_count, 1)])

    first = trial_vectors[:, :vectors]
    second = trial_vectors[:, vectors:]
    mine = jnp.where(core == 0, first, second)
    theirs = exchange(jnp.where(core == 0, second, first), "row", row_count, 1)
    panel = jnp.concatenate([mine, theirs])

    place = jnp.stack([chip, core, piece]).astype(jnp.int32)
    held = col_count // 2
    part = domain * width // 2
    columns = PAIR * per * width
    scalars = pl.BlockSpec(memory_space=pltpu.SMEM)
    vectors_spec = pl.BlockSpec(memory_space=pltpu.VMEM)
    matrices = [[None] * chips for _ in range(2)]
    sends = {}
    last = None
    for half in (1, 0):
        top = (piece // held) ^ half
        for step in (*range(1, chips), 0):
            at = PAIR * (chip ^ step)
            if last is not None:
                at, _ = lax.optimization_barrier((at, last))
            last = lax.dynamic_slice(raw, (at, top * part, 0), (PAIR, part, slots * width))
            sends[half, step] = last
    for half in (1, 0):
        for step in range(chips):
            sent = sends[half, step]
            same = sent if step == 0 else exchange(sent, "row", row_count, PAIR * step)
            other = exchange(same, "row", row_count, 1)
            matrices[half][step] = pl.pallas_call(
                functools.partial(place_blocks, step, per, width, half, col_count, row_count),
                out_shape=jax.ShapeDtypeStruct((PAIR * part, columns), jnp.bfloat16),
                in_specs=[scalars, scalars, vectors_spec, vectors_spec],
                out_specs=vectors_spec,
                cost_estimate=pl.CostEstimate(
                    flops=PAIR * part * columns * 3,
                    bytes_accessed=PAIR * part * columns * 4,
                    transcendentals=0,
                ),
                compiler_params=pltpu.CompilerParams(
                    vmem_limit_bytes=PAIR * part * (columns + 2 * slots * width) * 4 + (1 << 20)
                ),
            )(
                place,
                used,
                same.reshape(PAIR * part, slots * width),
                other.reshape(PAIR * part, slots * width),
            )

    centre_value = center[0]
    half_value = half_width[0]
    rows = domain * width // col_count
    span = PAIR * rows

    def operator(current):
        arrived = [current]
        for step in range(1, chips):
            arrived.append(exchange(current, "row", row_count, PAIR * step))
        parts = {}
        for half in (1, 0):
            total = None
            for step, (matrix, value) in enumerate(zip(matrices[half], arrived)):
                term = jnp.dot(matrix, value, preferred_element_type=jnp.float32)
                total = term if total is None else lax.optimization_barrier(total) + term
            for index in range(held):
                step = half * held + index
                value = total[index * span : (index + 1) * span]
                if step:
                    value = exchange(value.astype(jnp.bfloat16), "col", col_count, step)
                parts[step] = value
        owned = parts[0]
        for step in range(1, col_count):
            owned = owned + parts[step].astype(jnp.float32)
        return owned

    previous = panel.astype(jnp.float32)
    current = (operator(panel) - centre_value * previous) / half_value
    for _ in range(DEGREE - 1):
        product = operator(current.astype(jnp.bfloat16))
        following = 2.0 * (product - centre_value * current) / half_value - previous
        previous, current = (current, following)

    mine, theirs = current[:rows], exchange(current[rows:], "row", row_count, 1)
    return jnp.where(
        core == 0, jnp.concatenate([mine, theirs], 1), jnp.concatenate([theirs, mine], 1)
    )


def body(per, *arguments):
    return filter_body(per, *arguments)


def solution(mesh):
    in_specs = (
        P(("row", "col"), None),
        P("col", None, None, None, "row", None),
        P("col", "row", None, None, None),
        P("col", "row", None, None),
        P(),
        P(),
    )
    out_specs = P(("row", "col"), None)

    def whole(trial_vectors, h_blocks, block_col, block_count, center, half_width):
        shape = h_blocks.shape
        per = trial_vectors.shape[0] // (shape[0] * shape[4] * shape[3])
        return jax.shard_map(
            functools.partial(body, per), mesh=mesh, in_specs=in_specs, out_specs=out_specs, check_vma=False
        )(trial_vectors, h_blocks, block_col, block_count, center, half_width)

    return whole
```

```python
import functools

import jax
import jax.numpy as jnp
from jax import lax
from jax.experimental import pallas as pl
from jax.experimental.pallas import tpu as pltpu
from jax.sharding import PartitionSpec as P


DEGREE = 6
PAIR = 2
SLOTS = 2
UNROLL = 3


def exchange(value, axis, size, offset):
    return lax.ppermute(value, axis, [(i, i ^ offset) for i in range(size)])


def place_blocks(chips, per, width, half, pieces, sources, place, used, *refs):
    same, other, dense = refs[:chips], refs[chips : 2 * chips], refs[2 * chips :]
    chip, core, piece = place[0], place[1], place[2]
    lane = lax.broadcasted_iota(jnp.int32, (1, SLOTS * width), 1) < width
    held = pieces // 2
    count = dense[0].shape[0] // (held * PAIR * width)
    halves = [(far, column) for far in range(PAIR) for column in range(per)]

    def block_row(index, carry):
        row = lax.rem(index, count)
        near = lax.rem(index // count, PAIR)
        at = (piece ^ (index // (count * PAIR))) & (held - 1)
        base = (near * pieces + (at | (((piece // held) ^ half) * held))) * count + row
        source_row = pl.multiple_of(((core ^ near) * held + at) * count * width + row * width, width)
        target = pl.multiple_of(index * width, width)
        for step in range(chips):
            sides = []
            for far, ref in enumerate((same[step], other[step])):
                value = ref[pl.ds(source_row, width), :]
                source = PAIR * (chip ^ step) + (core ^ far)
                slots = [used[(base * sources + source) * SLOTS + slot] for slot in range(SLOTS)]
                sides.append((value, pltpu.roll(value, width, 1), slots))
            for tile in range(len(halves) // 2):
                (far_a, col_a), (far_b, col_b) = halves[2 * tile], halves[2 * tile + 1]
                terms = {}
                for far, turned, wanted, left in (
                    (far_a, 0, sides[far_a][2][0] == col_a, True),
                    (far_a, 1, sides[far_a][2][1] == col_a, True),
                    (far_b, 0, sides[far_b][2][1] == col_b, False),
                    (far_b, 1, sides[far_b][2][0] == col_b, False),
                ):
                    terms.setdefault((far, turned), {})[left] = wanted.astype(jnp.int32)
                result = None
                for (far, turned), wanted in terms.items():
                    factor = jnp.where(lane, wanted.get(True, 0), wanted.get(False, 0))
                    term = sides[far][turned] * factor.astype(jnp.float32).astype(dense[step].dtype)
                    result = term if result is None else result + term
                columns = pl.ds(tile * SLOTS * width, SLOTS * width)
                dense[step][pl.ds(target, width), columns] = result
        return carry

    lax.fori_loop(0, held * PAIR * count, block_row, 0, unroll=UNROLL)


def filter_body(per, trial_vectors, h_blocks, block_col, block_count, center, half_width):
    row_count = lax.axis_size("row")
    col_count = lax.axis_size("col")
    chips = row_count // PAIR
    row_index = lax.axis_index("row")
    chip, core = row_index // PAIR, row_index % PAIR
    piece = lax.axis_index("col")
    domain = h_blocks.shape[2]
    width = h_blocks.shape[3]
    slots = h_blocks.shape[5] // width
    vectors = trial_vectors.shape[1] // PAIR

    raw = h_blocks.reshape(row_count, domain * width, slots * width)
    used = jnp.where(
        lax.broadcasted_iota(jnp.int32, block_col.shape[2:], 2) < block_count[0, 0][:, :, None],
        block_col[0, 0],
        -1,
    ).reshape(-1)
    used = jnp.concatenate([used, exchange(used, "row", row_count, 1)])

    place = jnp.stack([chip, core, piece]).astype(jnp.int32)
    held = col_count // 2
    part = domain * width // 2
    columns = PAIR * per * width
    scalars = pl.BlockSpec(memory_space=pltpu.SMEM)
    vectors_spec = pl.BlockSpec(memory_space=pltpu.VMEM)
    order = gather_order(chips)
    first = trial_vectors[:, :vectors]
    second = trial_vectors[:, vectors:]
    mine = jnp.where(core == 0, first, second)
    theirs = exchange(jnp.where(core == 0, second, first), "row", row_count, 1)
    panel = jnp.concatenate([mine, theirs])
    sends = {}
    last = None
    for half in (1, 0):
        top = (piece // held) ^ half
        for step in (*order, 0):
            at = PAIR * (chip ^ step)
            if last is not None:
                at, _ = lax.optimization_barrier((at, last))
            last = lax.dynamic_slice(raw, (at, top * part, 0), (PAIR, part, slots * width))
            sends[half, step] = last.reshape(PAIR * part, slots * width)
    matrices = [None, None]
    for half in (1, 0):
        same, other = [], []
        for step in range(chips):
            sent = sends[half, step]
            same.append(sent if step == 0 else exchange(sent, "row", row_count, PAIR * step))
            other.append(exchange(same[step], "row", row_count, 1))
        matrices[half] = pl.pallas_call(
            functools.partial(place_blocks, chips, per, width, half, col_count, row_count),
            out_shape=[jax.ShapeDtypeStruct((PAIR * part, columns), jnp.bfloat16)] * chips,
            in_specs=[scalars, scalars] + [vectors_spec] * (2 * chips),
            out_specs=[vectors_spec] * chips,
            cost_estimate=pl.CostEstimate(
                flops=PAIR * part * columns * 3 * chips,
                bytes_accessed=PAIR * part * columns * 4 * chips,
                transcendentals=0,
            ),
            compiler_params=pltpu.CompilerParams(
                vmem_limit_bytes=chips * PAIR * part * (columns + 2 * slots * width) * 4 + (1 << 20)
            ),
        )(place, used, *same, *other)

    centre_value = center[0]
    half_value = half_width[0]
    rows = domain * width // col_count
    span = PAIR * rows

    def operator(current):
        arrived = [current]
        for step in range(1, chips):
            arrived.append(exchange(current, "row", row_count, PAIR * step))
        parts = {}
        for half in (1, 0):
            total = None
            for step in (0, *order):
                term = jnp.dot(
                    matrices[half][step], arrived[step], preferred_element_type=jnp.float32
                )
                total = term if total is None else lax.optimization_barrier(total) + term
            for index in range(held):
                step = half * held + index
                value = total[index * span : (index + 1) * span]
                if step:
                    value = exchange(value.astype(jnp.bfloat16), "col", col_count, step)
                parts[step] = value
        owned = parts[0]
        for step in range(1, col_count):
            owned = owned + parts[step].astype(jnp.float32)
        return owned

    previous = panel.astype(jnp.float32)
    current = (operator(panel) - centre_value * previous) / half_value
    for _ in range(DEGREE - 1):
        product = operator(current.astype(jnp.bfloat16))
        following = 2.0 * (product - centre_value * current) / half_value - previous
        previous, current = (current, following)

    mine, theirs = current[:rows], exchange(current[rows:], "row", row_count, 1)
    return jnp.where(
        core == 0, jnp.concatenate([mine, theirs], 1), jnp.concatenate([theirs, mine], 1)
    )


def body(per, *arguments):
    return filter_body(per, *arguments)


def gather_order(chips):
    return (chips - 1, *range(1, chips - 1))


def solution(mesh):
    in_specs = (
        P(("row", "col"), None),
        P("col", None, None, None, "row", None),
        P("col", "row", None, None, None),
        P("col", "row", None, None),
        P(),
        P(),
    )
    out_specs = P(("row", "col"), None)

    def whole(trial_vectors, h_blocks, block_col, block_count, center, half_width):
        shape = h_blocks.shape
        per = trial_vectors.shape[0] // (shape[0] * shape[4] * shape[3])
        return jax.shard_map(
            functools.partial(body, per), mesh=mesh, in_specs=in_specs, out_specs=out_specs, check_vma=False
        )(trial_vectors, h_blocks, block_col, block_count, center, half_width)

    return whole
```

```python
import functools

import jax
import jax.numpy as jnp
from jax import lax
from jax.experimental import pallas as pl
from jax.experimental.pallas import tpu as pltpu
from jax.sharding import PartitionSpec as P


DEGREE = 6
PAIR = 2
SLOTS = 2
UNROLL = 12


def exchange(value, axis, size, offset):
    return lax.ppermute(value, axis, [(i, i ^ offset) for i in range(size)])


def place_blocks(chips, per, width, half, pieces, sources, place, used, *refs):
    same, other, dense = refs[:chips], refs[chips : 2 * chips], refs[2 * chips :]
    chip, core, piece = place[0], place[1], place[2]
    lane = lax.broadcasted_iota(jnp.int32, (1, SLOTS * width), 1) < width
    held = pieces // 2
    count = dense[0].shape[0] // (held * PAIR * width)
    halves = [(far, column) for far in range(PAIR) for column in range(per)]

    def block_row(index, carry):
        row = lax.rem(index, count)
        near = lax.rem(index // count, PAIR)
        at = (piece ^ (index // (count * PAIR))) & (held - 1)
        base = (near * pieces + (at | (((piece // held) ^ half) * held))) * count + row
        source_row = pl.multiple_of(((core ^ near) * held + at) * count * width + row * width, width)
        target = pl.multiple_of(index * width, width)
        for step in range(chips):
            sides = []
            for far, ref in enumerate((same[step], other[step])):
                value = ref[pl.ds(source_row, width), :]
                source = PAIR * (chip ^ step) + (core ^ far)
                slots = [used[(base * sources + source) * SLOTS + slot] for slot in range(SLOTS)]
                sides.append((value, pltpu.roll(value, width, 1), slots))
            for tile in range(len(halves) // 2):
                (far_a, col_a), (far_b, col_b) = halves[2 * tile], halves[2 * tile + 1]
                terms = {}
                for far, turned, wanted, left in (
                    (far_a, 0, sides[far_a][2][0] == col_a, True),
                    (far_a, 1, sides[far_a][2][1] == col_a, True),
                    (far_b, 0, sides[far_b][2][1] == col_b, False),
                    (far_b, 1, sides[far_b][2][0] == col_b, False),
                ):
                    terms.setdefault((far, turned), {})[left] = wanted.astype(jnp.int32)
                result = None
                for (far, turned), wanted in terms.items():
                    factor = jnp.where(lane, wanted.get(True, 0), wanted.get(False, 0))
                    term = sides[far][turned] * factor.astype(jnp.float32).astype(dense[step].dtype)
                    result = term if result is None else result + term
                columns = pl.ds(tile * SLOTS * width, SLOTS * width)
                dense[step][pl.ds(target, width), columns] = result
        return carry

    lax.fori_loop(0, held * PAIR * count, block_row, 0, unroll=UNROLL)


def filter_body(per, trial_vectors, h_blocks, block_col, block_count, center, half_width):
    row_count = lax.axis_size("row")
    col_count = lax.axis_size("col")
    chips = row_count // PAIR
    row_index = lax.axis_index("row")
    chip, core = row_index // PAIR, row_index % PAIR
    piece = lax.axis_index("col")
    domain = h_blocks.shape[2]
    width = h_blocks.shape[3]
    slots = h_blocks.shape[5] // width
    vectors = trial_vectors.shape[1] // PAIR

    raw = h_blocks.reshape(row_count, domain * width, slots * width)
    used = jnp.where(
        lax.broadcasted_iota(jnp.int32, block_col.shape[2:], 2) < block_count[0, 0][:, :, None],
        block_col[0, 0],
        -1,
    ).reshape(-1)
    used = jnp.concatenate([used, exchange(used, "row", row_count, 1)])

    place = jnp.stack([chip, core, piece]).astype(jnp.int32)
    held = col_count // 2
    part = domain * width // 2
    columns = PAIR * per * width
    scalars = pl.BlockSpec(memory_space=pltpu.SMEM)
    vectors_spec = pl.BlockSpec(memory_space=pltpu.VMEM)
    order = gather_order(chips)
    first = trial_vectors[:, :vectors]
    second = trial_vectors[:, vectors:]
    mine = jnp.where(core == 0, first, second)
    theirs = exchange(jnp.where(core == 0, second, first), "row", row_count, 1)
    panel = jnp.concatenate([mine, theirs])
    sends = {}
    last = None
    for half in (1, 0):
        top = (piece // held) ^ half
        for step in (*order, 0):
            at = PAIR * (chip ^ step)
            if last is not None:
                at, _ = lax.optimization_barrier((at, last))
            last = lax.dynamic_slice(raw, (at, top * part, 0), (PAIR, part, slots * width))
            sends[half, step] = last.reshape(PAIR * part, slots * width)
    matrices = [None, None]
    for half in (1, 0):
        same, other = [], []
        for step in range(chips):
            sent = sends[half, step]
            same.append(sent if step == 0 else exchange(sent, "row", row_count, PAIR * step))
            other.append(exchange(same[step], "row", row_count, 1))
        matrices[half] = pl.pallas_call(
            functools.partial(place_blocks, chips, per, width, half, col_count, row_count),
            out_shape=[jax.ShapeDtypeStruct((PAIR * part, columns), jnp.bfloat16)] * chips,
            in_specs=[scalars, scalars] + [vectors_spec] * (2 * chips),
            out_specs=[vectors_spec] * chips,
            cost_estimate=pl.CostEstimate(
                flops=PAIR * part * columns * 3 * chips,
                bytes_accessed=PAIR * part * columns * 4 * chips,
                transcendentals=0,
            ),
            compiler_params=pltpu.CompilerParams(
                vmem_limit_bytes=chips * PAIR * part * (columns + 2 * slots * width) * 4 + (1 << 20)
            ),
        )(place, used, *same, *other)

    centre_value = center[0]
    half_value = half_width[0]
    rows = domain * width // col_count
    span = PAIR * rows

    def operator(number, current):
        arrived = [current]
        for step in range(1, chips):
            arrived.append(exchange(current, "row", row_count, PAIR * step))
        parts = {}
        for half in (1, 0):
            total = None
            for step in (0, *(order if number == 0 else range(1, chips))):
                term = jnp.dot(
                    matrices[half][step], arrived[step], preferred_element_type=jnp.float32
                )
                total = term if total is None else lax.optimization_barrier(total) + term
            for index in range(held):
                step = half * held + index
                value = total[index * span : (index + 1) * span]
                if step:
                    value = exchange(value.astype(jnp.bfloat16), "col", col_count, step)
                parts[step] = value
        owned = parts[0]
        for step in range(1, col_count):
            owned = owned + parts[step].astype(jnp.float32)
        return owned

    previous = panel.astype(jnp.float32)
    current = (operator(0, panel) - centre_value * previous) / half_value
    for degree_step in range(DEGREE - 1):
        product = operator(degree_step + 1, current.astype(jnp.bfloat16))
        following = 2.0 * (product - centre_value * current) / half_value - previous
        previous, current = (current, following)

    mine, theirs = current[:rows], exchange(current[rows:], "row", row_count, 1)
    return jnp.where(
        core == 0, jnp.concatenate([mine, theirs], 1), jnp.concatenate([theirs, mine], 1)
    )


def body(per, *arguments):
    return filter_body(per, *arguments)


def gather_order(chips):
    return tuple(range(1, chips))


def solution(mesh):
    in_specs = (
        P(("row", "col"), None),
        P("col", None, None, None, "row", None),
        P("col", "row", None, None, None),
        P("col", "row", None, None),
        P(),
        P(),
    )
    out_specs = P(("row", "col"), None)

    def whole(trial_vectors, h_blocks, block_col, block_count, center, half_width):
        shape = h_blocks.shape
        per = trial_vectors.shape[0] // (shape[0] * shape[4] * shape[3])
        return jax.shard_map(
            functools.partial(body, per), mesh=mesh, in_specs=in_specs, out_specs=out_specs, check_vma=False
        )(trial_vectors, h_blocks, block_col, block_count, center, half_width)

    return whole
```
